256 devices in a mesh: layer: 4 (over y), row: 4 (over x), col: 16 (over z, core).
Axes of the slice: x: 4, y: 4, z: 8, core: 2. Of those that a mesh axis runs over, the one named last changes fastest.
Arguments:
- root_rhs: bfloat16 [1024, 8192], P(('layer', 'col'), 'row'), may hold values from -6 to 6
- root_inverse: bfloat16 [8192, 8192], P('row', 'col'), may hold values from -0.0625 to 0.0625
- child_rhs: bfloat16 [4, 1024, 8192], P('layer', 'col', 'row'), may hold values from -6 to 6
- child_inverse: bfloat16 [4, 8192, 8192], P('layer', 'row', 'col'), may hold values from -0.0625 to 0.0625
- off_diagonal: bfloat16 [4, 8192, 8192], P('layer', 'col', 'row'), may hold values from -0.09375 to 0.09375
- pattern: int32 [4, 16, 16], P('layer'), may hold values 0 or 1
Outputs:
- root_solution: bfloat16 [1024, 8192], P(('layer', 'row'), 'col')
- child_solution: bfloat16 [4, 1024, 8192], P('layer', 'row', 'col')
The draws below stay inside these ranges and needn't reach their ends.
All inputs are finite; a program needn't handle non-finite values. No bound on the sum of `pattern` on one device may be relied on, other than what follows from the above.
Results may differ from the reference program's by a relative error of at most 0.019.
Values may be sent and summed in bfloat16 or wider, within the bound.
No kernel may reach another device: no remote copies, remote signals or barrier semaphores. Data moves between devices by JAX's collectives and lax.ppermute only.
A program may use at most 64 MiB of HBM per device.

```python
import jax
import jax.numpy as jnp

R = 8192
C = 8192
K = 1024
BR = 16
BC = 16
NCH = 4


def set_ends(array, rng, low, high):
    shape = array.shape
    spot = [jax.random.randint(jax.random.fold_in(rng, axis), (), 0, shape[axis]) for axis in range(len(shape))]
    array = array.at[tuple(spot)].set(low)
    longest = shape.index(max(shape))
    spot[longest] = (spot[longest] + 1) % shape[longest]
    return array.at[tuple(spot)].set(high)


def block_levels(key, extent, pieces, low, high):
    def one(dim, blocks):
        heights = jax.random.uniform(jax.random.fold_in(jax.random.fold_in(key, 6), dim), (blocks,), jnp.float32, low / len(pieces), high / len(pieces))
        return jnp.repeat(jnp.exp(heights), extent[dim] // blocks).reshape((-1,) + (1,) * (len(extent) - dim - 1))

    loudness = one(*pieces[0])
    for cut in pieces[1:]:
        loudness = loudness * one(*cut)
    return loudness


def centred(rng, dims, width, limit, pieces=(), held_as=jnp.bfloat16):
    result = jax.random.normal(rng, dims, jnp.float32) * width
    if len(pieces) > 0:
        result = block_levels(rng, dims, pieces, -0.22, 0.18) * result
    return jnp.clip(result, min=-limit, max=limit).astype(held_as)


def setup_inputs(seed: int = 0) -> dict:
    seeds = jax.random.split(jax.random.key(seed), 7)
    root_rhs = centred(seeds[0], (K, R), 1.0, 6.0, ((0, 64), (1, 4)))
    root_inverse = centred(seeds[1], (R, R), R ** -0.5, 0.0625, ((0, 4), (1, 16)))
    child_rhs = centred(seeds[2], (NCH, K, C), 1.0, 6.0, ((0, 4), (1, 16), (2, 4)))
    child_inverse = centred(seeds[3], (NCH, C, C), C ** -0.5, 0.0625, ((0, 4), (1, 4), (2, 16)))
    off_diagonal = centred(seeds[4], (NCH, R, C), (R // 2) ** -0.5, 0.09375, ((0, 4), (1, 16), (2, 4)))
    pattern = set_ends((jax.random.randint(seeds[5], (NCH, BR, BC), 0, 2) < 1).astype(jnp.int32), jax.random.fold_in(seeds[5], 1), 0, 1)
    return {"root_rhs": root_rhs, "root_inverse": root_inverse, "child_rhs": child_rhs, "child_inverse": child_inverse, "off_diagonal": off_diagonal, "pattern": pattern}


def child_front(root_solution, rhs_block, inverse_block, coupling, block_mask):
    block_rows = R // BR
    block_cols = C // BC
    masked = (coupling.reshape(BR, block_rows, BC, block_cols) * block_mask.astype(jnp.bfloat16)[:, None, :, None]).reshape(R, C)
    update = jnp.dot(root_solution, masked, preferred_element_type=jnp.float32)
    reduced = (rhs_block.astype(jnp.float32) - update).astype(jnp.bfloat16)
    return jnp.dot(reduced, inverse_block, preferred_element_type=jnp.float32).astype(jnp.bfloat16)


def reference(root_rhs, root_inverse, child_rhs, child_inverse, off_diagonal, pattern):
    root_solution = jnp.dot(root_rhs, root_inverse, preferred_element_type=jnp.float32).astype(jnp.bfloat16)
    solutions = []
    for child_index in range(NCH):
        solutions.append(child_front(root_solution, child_rhs[child_index], child_inverse[child_index], off_diagonal[child_index], pattern[child_index]))
    return root_solution, jnp.stack(solutions, axis=0)
```

```python
import jax
import jax.numpy as jnp
from jax import lax
from jax.sharding import PartitionSpec as P


BF = jnp.bfloat16
F32 = jnp.float32
NZ = 8
NX = 4
BC = 16


def to_core(x):
    return lax.ppermute(x, "col", [(i, i ^ 1) for i in range(2 * NZ)])


def along_z(x, step):
    return lax.ppermute(x, "col", [(i, (i + 2 * step) % (2 * NZ)) for i in range(2 * NZ)])


def along(x, axis, step):
    return lax.ppermute(x, axis, [(i, (i + step) % NX) for i in range(NX)])


def pick(x, index):
    return lax.dynamic_index_in_dim(x, index, 0, keepdims=False)


def put(x, piece, index):
    return lax.dynamic_update_index_in_dim(x, piece, index, 0)


def dot(a, b):
    return jnp.dot(a, b, preferred_element_type=F32)


def gather_z(own, z, forward, backward):
    full = jnp.zeros((NZ,) + own.shape, own.dtype)
    full = put(full, own, z)
    up = down = own
    for step in range(1, max(forward, backward) + 1):
        if step <= forward:
            up = along_z(up, 1)
            full = put(full, up, (z - step) % NZ)
        if step <= backward:
            down = along_z(down, -1)
            full = put(full, down, (z + step) % NZ)
    return full


def scatter_z(parts, z, forward, backward):
    up = down = None
    for step in range(max(forward, backward)):
        if step < forward:
            term = pick(parts, (z + forward - step) % NZ)
            term = term if up is None else term + up.astype(F32)
            up = along_z(term.astype(BF), 1)
        if step < backward:
            term = pick(parts, (z - backward + step) % NZ)
            term = term if down is None else term + down.astype(F32)
            down = along_z(term.astype(BF), -1)
    return pick(parts, z) + (up.astype(F32) + down.astype(F32))


def scatter_x(parts, r):
    total = pick(parts, r)
    for step in (1, 2, 3):
        piece = along(pick(parts, (r + step) % NX).astype(BF), "row", step)
        total = total + piece.astype(F32)
    return total.astype(BF)


def gather_axis(own, axis, me):
    full = jnp.zeros((NX,) + own.shape, own.dtype)
    full = put(full, own, me)
    for step in (1, 2, 3):
        full = put(full, along(own, axis, step), (me - step) % NX)
    return full


def on_device(root_rhs, root_inverse, child_rhs, child_inverse, off_diagonal, pattern):
    layer = lax.axis_index("layer")
    r = lax.axis_index("row")
    k = lax.axis_index("col")
    z = k // 2
    c = k % 2
    first = c == 0

    height, breadth = off_diagonal.shape[1:]
    half = breadth // 2
    blocks = BC // NX
    mask = lax.dynamic_slice(pattern[0], (k, r * blocks), (1, blocks)).astype(BF)
    masked = (
        off_diagonal[0].reshape(height, blocks, breadth // blocks) * mask[0][None, :, None]
    ).reshape(height, breadth)
    couple_own = lax.dynamic_slice(masked, (0, c * half), (height, half))
    couple_far = to_core(lax.dynamic_slice(masked, (0, (1 - c) * half), (height, half)))
    rows = child_rhs.shape[1]
    rhs_own = lax.dynamic_slice(child_rhs[0], (0, c * half), (rows, half))
    rhs_far = to_core(lax.dynamic_slice(child_rhs[0], (0, (1 - c) * half), (rows, half)))
    rhs = (jnp.where(first, rhs_own, rhs_far), jnp.where(first, rhs_far, rhs_own))
    width = child_inverse.shape[2]
    inverse_own = lax.dynamic_slice(child_inverse[0], (c * half, 0), (half, width))
    inverse_far = lax.dynamic_slice(child_inverse[0], ((1 - c) * half, 0), (half, width))

    x_own = gather_z(root_rhs, z, 4, 3)
    x_far = to_core(x_own)
    small, depth = root_rhs.shape
    s_own = dot(x_own.reshape(NZ * small, depth), root_inverse)
    s_far = dot(x_far.reshape(NZ * small, depth), root_inverse)
    s_all = jnp.stack([jnp.where(first, s_own, s_far), jnp.where(first, s_far, s_own)])
    s_all = s_all.reshape(2, NX, 2, small, width).transpose(1, 2, 0, 3, 4).reshape(NX, rows, width)
    solved = scatter_x(s_all, r)

    full = gather_axis(gather_axis(solved, "row", r), "layer", layer)
    full_far = to_core(full)
    full = full.reshape(NZ, 2, rows, width)
    full_far = full_far.reshape(NZ, 2, rows, width)

    outs = []
    for h in range(2):
        ahead, back = (4, 3) if h == 0 else (3, 4)
        update = dot(full[:, h].reshape(NZ * rows, width), couple_own) + dot(
            full_far[:, h].reshape(NZ * rows, width), couple_far
        )
        update = scatter_z(update.reshape(NZ, rows, half), z, ahead, back)
        reduced = (rhs[h].astype(F32) - update).astype(BF)
        near = gather_z(reduced, z, ahead, back)
        far = to_core(near)
        part = dot(near.reshape(NZ * rows, half), inverse_own) + dot(
            far.reshape(NZ * rows, half), inverse_far
        )
        outs.append(scatter_x(part.reshape(NX, 2, rows, width), r))
    child = jnp.stack(outs, axis=1).reshape(1, 4 * rows, width)
    return (solved, child)


def solution(mesh):
    in_specs = (
        P(("layer", "col"), "row"),
        P("row", "col"),
        P("layer", "col", "row"),
        P("layer", "row", "col"),
        P("layer", "col", "row"),
        P("layer", None, None),
    )
    out_specs = (P(("layer", "row"), "col"), P("layer", "row", "col"))
    return jax.shard_map(
        on_device, mesh=mesh, in_specs=in_specs, out_specs=out_specs, check_vma=False
    )
```

```python
import jax
import jax.numpy as jnp
from jax import lax
from jax.sharding import PartitionSpec as P


BF = jnp.bfloat16
F32 = jnp.float32
NZ = 8
NX = 4
BC = 16


def to_core(x):
    return lax.ppermute(x, "col", [(i, i ^ 1) for i in range(2 * NZ)])


def along_z(x, step):
    return lax.ppermute(x, "col", [(i, (i + 2 * step) % (2 * NZ)) for i in range(2 * NZ)])


def twisted(x, step):
    pairs = []
    for i in range(2 * NZ):
        z, c = i // 2, i % 2
        pairs.append((i, 2 * ((z + (step if c == 0 else -step)) % NZ) + c))
    return lax.ppermute(x, "col", pairs)


def exchange(x, axes):
    return lax.all_to_all(x, axes, 0, 0, tiled=True)


def pick(x, index):
    return lax.dynamic_index_in_dim(x, index & (NZ - 1), 0, keepdims=False)


def put(x, piece, index):
    return lax.dynamic_update_index_in_dim(x, piece, index & (NZ - 1), 0)


def dot(a, b):
    return jnp.dot(a, b, preferred_element_type=F32)


def on_device(root_rhs, root_inverse, child_rhs, child_inverse, off_diagonal, pattern):
    r = lax.axis_index("row")
    k = lax.axis_index("col")
    z = k >> 1
    c = k & 1
    first = c == 0
    sign = 1 - 2 * c

    height, breadth = off_diagonal.shape[1:]
    half = breadth // 2
    blocks = BC // NX
    rows = child_rhs.shape[1]
    width = child_inverse.shape[2]
    small, depth = root_rhs.shape

    x_own = put(jnp.zeros((NZ, small, depth), BF), root_rhs, z)
    up, down = along_z(root_rhs, 1), along_z(root_rhs, -1)
    x_own = put(put(x_own, up, z - 1), down, z + 1)

    mask = lax.dynamic_slice(pattern[0], (k, r * blocks), (1, blocks)).astype(BF)
    masked = (
        off_diagonal[0].reshape(height, blocks, breadth // blocks) * mask[0][None, :, None]
    ).reshape(height, breadth)
    couple_own = lax.dynamic_slice(masked, (0, c * half), (height, half))
    couple_out = lax.dynamic_slice(masked, (0, (1 - c) * half), (height, half))
    rhs_own = lax.dynamic_slice(child_rhs[0], (0, c * half), (rows, half))
    rhs_out = lax.dynamic_slice(child_rhs[0], (0, (1 - c) * half), (rows, half))
    inverse_own = lax.dynamic_slice(child_inverse[0], (c * half, 0), (half, width))
    inverse_far = lax.dynamic_slice(child_inverse[0], ((1 - c) * half, 0), (half, width))

    up, down = along_z(up, 1), along_z(down, -1)
    x_own = put(put(x_own, up, z - 2), down, z + 2)
    up, down, couple_out, rhs_out, couple_own, inverse_own, inverse_far = lax.optimization_barrier(
        (up, down, couple_out, rhs_out, couple_own, inverse_own, inverse_far)
    )
    up, down = along_z(up, 1), along_z(down, -1)
    couple_far = to_core(couple_out)
    rhs_far = to_core(rhs_out)
    x_own = put(put(x_own, up, z - 3), down, z + 3)
    up, couple_far, rhs_far = lax.optimization_barrier((up, couple_far, rhs_far))
    up = along_z(up, 1)
    x_own = put(x_own, up, z - 4)
    x_far = to_core(x_own)
    rhs = jnp.stack([jnp.where(first, rhs_own, rhs_far), jnp.where(first, rhs_far, rhs_own)])
    rhs = rhs.reshape(2 * rows, half)

    s_own = dot(x_own.reshape(NZ * small, depth), root_inverse)
    s_far = dot(x_far.reshape(NZ * small, depth), root_inverse)
    s_all = jnp.stack([jnp.where(first, s_own, s_far), jnp.where(first, s_far, s_own)]).astype(BF)
    s_all = s_all.reshape(2, NX, 2, small, width).transpose(1, 2, 0, 3, 4).reshape(NX, rows, width)
    solved = exchange(s_all, "row").astype(F32).sum(0).astype(BF)

    full = exchange(jnp.broadcast_to(solved[None], (NX * NX, rows, width)), ("layer", "row"))
    full = full.reshape(NX * NX * rows, width)
    full_far = to_core(full)
    update = (dot(full, couple_own) + dot(full_far, couple_far)).astype(BF)
    update = update.reshape(NZ, 2 * rows, half)

    distant = pick(update, z + 4)
    up = twisted(distant[:rows], 1)
    down = twisted(distant[rows:], -1)
    for step in (3, 2, 1):
        ahead = pick(update, z + sign * step).astype(F32)
        behind = pick(update, z - sign * step).astype(F32)
        up, down = up.astype(F32), down.astype(F32)
        if step == 3:
            ahead = jnp.concatenate([ahead[:rows] + up, ahead[rows:]])
            behind = jnp.concatenate([behind[:rows], behind[rows:] + down])
        else:
            ahead, behind = ahead + up, behind + down
        up = twisted(lax.optimization_barrier(ahead.astype(BF)), 1)
        down = twisted(lax.optimization_barrier(behind.astype(BF)), -1)
    total = pick(update, z).astype(F32) + (up.astype(F32) + down.astype(F32))
    reduced = (rhs.astype(F32) - total).astype(BF)

    near = put(jnp.zeros((NZ, 2 * rows, half), BF), reduced, z)
    up = down = reduced
    for step in (1, 2, 3):
        up, down = twisted(up, 1), twisted(down, -1)
        near = put(put(near, up, z - sign * step), down, z + sign * step)
    up, down = twisted(up[:rows], 1), twisted(down[rows:], -1)
    near = put(near, jnp.concatenate([up, down]), z + 4)
    near = near.reshape(2 * NZ * rows, half)
    far = to_core(near)
    part = (dot(near, inverse_own) + dot(far, inverse_far)).astype(BF)
    child = exchange(part.reshape(NX, 4 * rows, width), "row").astype(F32).sum(0).astype(BF)
    return (solved, child[None])


def solution(mesh):
    in_specs = (
        P(("layer", "col"), "row"),
        P("row", "col"),
        P("layer", "col", "row"),
        P("layer", "row", "col"),
        P("layer", "col", "row"),
        P("layer", None, None),
    )
    out_specs = (P(("layer", "row"), "col"), P("layer", "row", "col"))
    return jax.shard_map(
        on_device, mesh=mesh, in_specs=in_specs, out_specs=out_specs, check_vma=False
    )
```

```python
import jax
import jax.numpy as jnp
from jax import lax
from jax.experimental import pallas as pl
from jax.experimental.pallas import tpu as pltpu
from jax.sharding import PartitionSpec as P


BF = jnp.bfloat16
F32 = jnp.float32
NZ = 8
NX = 4
BC = 16
REACH = ((4, 3), (3, 4))


def to_core(x):
    return lax.ppermute(x, "col", [(i, i ^ 1) for i in range(2 * NZ)])


def twisted(x, step=1):
    pairs = []
    for i in range(2 * NZ):
        z, c = i // 2, i % 2
        pairs.append((i, 2 * ((z + (step if c == 0 else -step)) % NZ) + c))
    return lax.ppermute(x, "col", pairs)


def along_z(x, step):
    return lax.ppermute(x, "col", [(i, (i + 2 * step) % (2 * NZ)) for i in range(2 * NZ)])


def exchange(x, axes):
    return lax.all_to_all(x, axes, 0, 0, tiled=True)


def pick(x, index):
    return lax.dynamic_index_in_dim(x, index, 0, keepdims=False)


def put(x, piece, index):
    return lax.dynamic_update_index_in_dim(x, piece, index, 0)


def dot(a, b):
    return jnp.dot(a, b, preferred_element_type=F32)


def root_kernel(at, home, one, two, three, four, f12, f34, a, out, x):
    z, c = at[0], at[1]
    sign = 1 - 2 * c
    n = home.shape[0]
    h = n // 2

    def place(value, chip, core):
        start = pl.multiple_of((chip & (NZ - 1)) * n + core * h, h)
        x[pl.ds(start, h), :] = value

    def pair(ref, start, chip, core):
        place(ref[start : start + h, :], chip, core)
        place(ref[start + h : start + n, :], chip, 1 - core)

    pair(home, 0, z, c)
    pair(one, 0, z - sign, c)
    pair(two, 0, z - 2 * sign, c)
    pair(three, 0, z - 3 * sign, c)
    place(four[...], z + 4, c)
    pair(f12, 0, z + sign, 1 - c)
    pair(f12, n, z + 2 * sign, 1 - c)
    pair(f34, 0, z + 3 * sign, 1 - c)
    place(f34[n:, :], z + 4, 1 - c)
    out[...] = dot(x[...], a[...]).astype(BF)


def child_product(c, near, far, inverse):
    depth = near.shape[1]
    own_rows = pl.ds(pl.multiple_of(c * depth, depth), depth)
    far_rows = pl.ds(pl.multiple_of((1 - c) * depth, depth), depth)
    return (dot(near[...], inverse[own_rows, :]) + dot(far[...], inverse[far_rows, :])).astype(BF)


def first_kernel(at, near, far, inverse, out):
    out[...] = child_product(at[1], near, far, inverse)


def second_kernel(at, near, far, inverse, before, out):
    block = child_product(at[1], near, far, inverse)
    n = before.shape[0] // NZ
    for i in range(NZ):
        out[2 * i * n : (2 * i + 1) * n, :] = before[i * n : (i + 1) * n, :]
        out[(2 * i + 1) * n : (2 * i + 2) * n, :] = block[i * n : (i + 1) * n, :]


def local_call(kernel, rows, width, inputs, flops, scratch=()):
    vmem = pl.BlockSpec(memory_space=pltpu.VMEM)
    size = sum(x.size * x.dtype.itemsize for x in inputs)
    return pl.pallas_call(
        kernel,
        out_shape=jax.ShapeDtypeStruct((rows, width), BF),
        in_specs=[pl.BlockSpec(memory_space=pltpu.SMEM)] + [vmem] * (len(inputs) - 1),
        out_specs=vmem,
        scratch_shapes=scratch,
        compiler_params=pltpu.CompilerParams(vmem_limit_bytes=16 * 2**20),
        cost_estimate=pl.CostEstimate(
            flops=flops, bytes_accessed=size + 2 * rows * width, transcendentals=0
        ),
    )(*inputs)


def on_device(root_rhs, root_inverse, child_rhs, child_inverse, off_diagonal, pattern):
    r = lax.axis_index("row")
    k = lax.axis_index("col")
    z = k >> 1
    c = k & 1
    first = c == 0

    height, breadth = off_diagonal.shape[1:]
    half = breadth // 2
    blocks = BC // NX
    rows = child_rhs.shape[1]
    width = child_inverse.shape[2]
    small, depth = root_rhs.shape

    other = to_core(root_rhs)
    home = jnp.concatenate([root_rhs, other])
    four = twisted(home[:small], 4)
    three = twisted(home, 3)
    two = twisted(home, 2)
    one = twisted(home, 1)
    couple_own = lax.dynamic_slice(off_diagonal[0], (0, c * half), (height, half))
    couple_out = lax.dynamic_slice(off_diagonal[0], (0, (1 - c) * half), (height, half))
    rhs_own = lax.dynamic_slice(child_rhs[0], (0, c * half), (rows, half))
    rhs_out = lax.dynamic_slice(child_rhs[0], (0, (1 - c) * half), (rows, half))
    f43 = to_core(jnp.concatenate([three, four]))
    f12 = to_core(jnp.concatenate([one, two]))
    couple_far, rhs_far = to_core(couple_out), to_core(rhs_out)
    f12, couple_far, rhs_far, couple_own = lax.optimization_barrier(
        (f12, couple_far, rhs_far, couple_own)
    )
    rhs = (jnp.where(first, rhs_own, rhs_far), jnp.where(first, rhs_far, rhs_own))
    masks = lax.dynamic_slice(pattern[0], (2 * z, r * blocks + c * (blocks // 2)), (2, blocks // 2))
    masks = jnp.repeat(masks != 0, half // (blocks // 2), axis=1)
    keep_own = jnp.where(first, masks[0], masks[1])
    keep_far = jnp.where(first, masks[1], masks[0])
    at = jnp.stack([z, c]).astype(jnp.int32)
    part = local_call(
        root_kernel,
        2 * NZ * small,
        width,
        (at, home, one, two, three, four, f12, f43, root_inverse),
        4 * NZ * small * depth * width,
        [pltpu.VMEM((2 * NZ * small, depth), BF)],
    )

    solved = exchange(part.reshape(NX, rows, width), "row").astype(F32).sum(0).astype(BF)
    full = jnp.broadcast_to(solved[None], (NX * NX, rows, width))
    full = exchange(full, ("layer", "row")).reshape(NX * NX * rows, width)
    full_far = to_core(full)
    update = jnp.where(keep_own[None], dot(full, couple_own), 0.0) + jnp.where(
        keep_far[None], dot(full_far, couple_far), 0.0
    )
    update = update.astype(BF).reshape(2 * NZ, rows, half)

    def term(h, d):
        return lax.optimization_barrier(pick(update, 2 * ((z + d) & (NZ - 1)) + h))

    terms = {(h, d): term(h, d) for h in range(2) for d in range(-REACH[h][1], REACH[h][0] + 1)}
    chains = {}
    for step in range(4):
        for h in range(2):
            for way, n in zip((1, -1), REACH[h]):
                if step < n:
                    block = terms[h, way * (n - step)]
                    if step > 0:
                        block = (block.astype(F32) + chains[h, way].astype(F32)).astype(BF)
                    chains[h, way] = along_z(block, way)

    near = []
    for h in range(2):
        base = rhs[h].astype(F32) - terms[h, 0].astype(F32)
        reduced = (base - (chains[h, 1].astype(F32) + chains[h, -1].astype(F32))).astype(BF)
        near.append(put(jnp.zeros((NZ, rows, half), BF), reduced, z))
        chains[h, 1] = chains[h, -1] = reduced
    for step in range(4):
        for h in range(2):
            for way, n in zip((1, -1), REACH[h]):
                if step < n:
                    chains[h, way] = along_z(chains[h, way], way)
                    near[h] = put(near[h], chains[h, way], (z - way * (step + 1)) & (NZ - 1))

    part = ()
    for h, kernel in enumerate((first_kernel, second_kernel)):
        gathered = near[h].reshape(NZ * rows, half)
        far = to_core(gathered)
        part = (
            local_call(
                kernel,
                (h + 1) * NZ * rows,
                width,
                (at, gathered, far, child_inverse[0], *part),
                4 * NZ * rows * half * width,
            ),
        )
    total = exchange(part[0].reshape(NX, 4 * rows, width), "row")
    child = total.astype(F32).sum(0).astype(BF)
    return (solved, child[None])


def solution(mesh):
    in_specs = (
        P(("layer", "col"), "row"),
        P("row", "col"),
        P("layer", "col", "row"),
        P("layer", "row", "col"),
        P("layer", "col", "row"),
        P("layer", None, None),
    )
    out_specs = (P(("layer", "row"), "col"), P("layer", "row", "col"))

    return jax.shard_map(
        on_device, mesh=mesh, in_specs=in_specs, out_specs=out_specs, check_vma=False
    )
```

```python
import jax
import jax.numpy as jnp
from jax import lax
from jax.experimental import pallas as pl
from jax.experimental.pallas import tpu as pltpu
from jax.sharding import PartitionSpec as P


BF = jnp.bfloat16
F32 = jnp.float32
NZ = 8
NX = 4
BC = 16
REACH = ((4, 3), (3, 4))


def to_core(x):
    return lax.ppermute(x, "col", [(i, i ^ 1) for i in range(2 * NZ)])


def twisted(x, step=1):
    pairs = []
    for i in range(2 * NZ):
        z, c = i // 2, i % 2
        pairs.append((i, 2 * ((z + (step if c == 0 else -step)) % NZ) + c))
    return lax.ppermute(x, "col", pairs)


def along_z(x, step):
    return lax.ppermute(x, "col", [(i, (i + 2 * step) % (2 * NZ)) for i in range(2 * NZ)])


def along_x(x, step):
    return lax.ppermute(x, "row", [(i, (i + step) % NX) for i in range(NX)])


def exchange(x, axes):
    return lax.all_to_all(x, axes, 0, 0, tiled=True)


def pick(x, index):
    return lax.dynamic_index_in_dim(x, index, 0, keepdims=False)


def put(x, piece, index):
    return lax.dynamic_update_index_in_dim(x, piece, index, 0)


def dot(a, b):
    return jnp.dot(a, b, preferred_element_type=F32)


def root_kernel(at, home, one, two, three, four, others, a, out, x):
    z, c = at[0], at[1]
    sign = 1 - 2 * c
    n = home.shape[0]
    h = n // 2

    def place(value, chip, core):
        start = pl.multiple_of((chip & (NZ - 1)) * n + core * h, h)
        x[pl.ds(start, h), :] = value

    def pair(ref, start, chip, core):
        place(ref[start : start + h, :], chip, core)
        place(ref[start + h : start + n, :], chip, 1 - core)

    pair(home, 0, z, c)
    pair(one, 0, z - sign, c)
    pair(two, 0, z - 2 * sign, c)
    pair(three, 0, z - 3 * sign, c)
    place(four[...], z + 4, c)
    for i in range(3):
        pair(others, i * n, z + (i + 1) * sign, 1 - c)
    place(others[3 * n :, :], z + 4, 1 - c)
    out[...] = dot(x[...], a[...]).astype(BF)


def child_product(c, near, far, inverse):
    depth = near.shape[1]
    own_rows = pl.ds(pl.multiple_of(c * depth, depth), depth)
    far_rows = pl.ds(pl.multiple_of((1 - c) * depth, depth), depth)
    return (dot(near[...], inverse[own_rows, :]) + dot(far[...], inverse[far_rows, :])).astype(BF)


def first_kernel(at, near, far, inverse, out):
    out[...] = child_product(at[1], near, far, inverse)


def second_kernel(at, near, far, inverse, before, *refs):
    outs, whole = refs[:NX], refs[NX]
    block = child_product(at[1], near, far, inverse)
    n = before.shape[0] // NZ
    for i in range(NZ):
        whole[2 * i * n : (2 * i + 1) * n, :] = before[i * n : (i + 1) * n, :]
        whole[(2 * i + 1) * n : (2 * i + 2) * n, :] = block[i * n : (i + 1) * n, :]
    size = whole.shape[0] // NX
    for d in range(NX):
        start = pl.multiple_of(((at[2] + d) & (NX - 1)) * size, size)
        outs[d][...] = whole[pl.ds(start, size), :]


def local_call(kernel, shapes, inputs, flops, scratch=()):
    vmem = pl.BlockSpec(memory_space=pltpu.VMEM)
    shapes = [jax.ShapeDtypeStruct(shape, BF) for shape in shapes]
    size = sum(x.size * x.dtype.itemsize for x in (*inputs, *shapes))
    return pl.pallas_call(
        kernel,
        out_shape=shapes,
        in_specs=[pl.BlockSpec(memory_space=pltpu.SMEM)] + [vmem] * (len(inputs) - 1),
        out_specs=[vmem] * len(shapes),
        scratch_shapes=scratch,
        compiler_params=pltpu.CompilerParams(vmem_limit_bytes=16 * 2**20),
        cost_estimate=pl.CostEstimate(flops=flops, bytes_accessed=size, transcendentals=0),
    )(*inputs)


def on_device(root_rhs, root_inverse, child_rhs, child_inverse, off_diagonal, pattern):
    r = lax.axis_index("row")
    k = lax.axis_index("col")
    z = k >> 1
    c = k & 1
    first = c == 0

    height, breadth = off_diagonal.shape[1:]
    half = breadth // 2
    blocks = BC // NX
    rows = child_rhs.shape[1]
    width = child_inverse.shape[2]
    small, depth = root_rhs.shape

    other = to_core(root_rhs)
    home = jnp.concatenate([root_rhs, other])
    four = twisted(home[:small], 4)
    three = twisted(home, 3)
    two = twisted(home, 2)
    one = twisted(home, 1)
    couple_own = lax.dynamic_slice(off_diagonal[0], (0, c * half), (height, half))
    rhs_own = lax.dynamic_slice(child_rhs[0], (0, c * half), (rows, half))
    away = jnp.concatenate(
        [
            lax.dynamic_slice(off_diagonal[0], (0, (1 - c) * half), (height, half)),
            lax.dynamic_slice(child_rhs[0], (0, (1 - c) * half), (rows, half)),
        ]
    )
    away = to_core(away)
    others = to_core(jnp.concatenate([one, two, three, four]))
    others, away, couple_own, rhs_own = lax.optimization_barrier((others, away, couple_own, rhs_own))
    couple_far, rhs_far = away[:height], away[height:]
    rhs = lax.optimization_barrier(
        (jnp.where(first, rhs_own, rhs_far), jnp.where(first, rhs_far, rhs_own))
    )
    masks = lax.dynamic_slice(pattern[0], (2 * z, r * blocks + c * (blocks // 2)), (2, blocks // 2))
    masks = jnp.repeat(masks != 0, half // (blocks // 2), axis=1)
    keep_own = jnp.where(first, masks[0], masks[1])
    keep_far = jnp.where(first, masks[1], masks[0])
    at = jnp.stack([z, c, r]).astype(jnp.int32)
    (part,) = local_call(
        root_kernel,
        [(2 * NZ * small, width)],
        (at, home, one, two, three, four, others, root_inverse),
        4 * NZ * small * depth * width,
        [pltpu.VMEM((2 * NZ * small, depth), BF)],
    )

    solved = exchange(part.reshape(NX, rows, width), "row").astype(F32).sum(0).astype(BF)
    full = jnp.broadcast_to(solved[None], (NX * NX, rows, width))
    full = exchange(full, ("layer", "row")).reshape(NX * NX * rows, width)
    full_far = to_core(full)
    update = lax.optimization_barrier(
        jnp.where(keep_own[None], dot(full, couple_own), 0.0).astype(BF)
    ).astype(F32) + jnp.where(keep_far[None], dot(full_far, couple_far), 0.0)
    update = update.astype(BF).reshape(2 * NZ, rows, half)

    def term(h, d):
        return lax.optimization_barrier(pick(update, 2 * ((z + d) & (NZ - 1)) + h))

    terms = {(h, d): term(h, d) for h in range(2) for d in range(-REACH[h][1], REACH[h][0] + 1)}
    chains = {}
    for step in range(4):
        for h in range(2):
            for way, n in zip((1, -1), REACH[h]):
                if step < n:
                    block = terms[h, way * (n - step)]
                    if step > 0:
                        block = (block.astype(F32) + chains[h, way].astype(F32)).astype(BF)
                    chains[h, way] = along_z(block, way)

    near = []
    for h in range(2):
        base = lax.optimization_barrier(rhs[h].astype(F32) - terms[h, 0].astype(F32))
        reduced = (base - (chains[h, 1].astype(F32) + chains[h, -1].astype(F32))).astype(BF)
        near.append(put(jnp.zeros((NZ, rows, half), BF), reduced, z))
        chains[h, 1] = chains[h, -1] = reduced
    for step in range(4):
        for h in range(2):
            for way, n in zip((1, -1), REACH[h]):
                if step < n:
                    chains[h, way] = along_z(chains[h, way], way)
                    near[h] = put(near[h], chains[h, way], (z - way * (step + 1)) & (NZ - 1))

    calls = (
        (first_kernel, [(NZ * rows, width)], ()),
        (second_kernel, [(4 * rows, width)] * NX, [pltpu.VMEM((2 * NZ * rows, width), BF)]),
    )
    parts = ()
    for h, (kernel, shapes, scratch) in enumerate(calls):
        gathered = near[h].reshape(NZ * rows, half)
        far = to_core(gathered)
        parts = local_call(
            kernel,
            shapes,
            (at, gathered, far, child_inverse[0], *parts),
            4 * NZ * rows * half * width,
            scratch,
        )
    total = parts[0].astype(F32)
    for step in (2, 1, 3):
        total = total + along_x(parts[step], step).astype(F32)
    child = total.astype(BF)
    return (solved, child[None])


def solution(mesh):
    in_specs = (
        P(("layer", "col"), "row"),
        P("row", "col"),
        P("layer", "col", "row"),
        P("layer", "row", "col"),
        P("layer", "col", "row"),
        P("layer", None, None),
    )
    out_specs = (P(("layer", "row"), "col"), P("layer", "row", "col"))

    return jax.shard_map(
        on_device, mesh=mesh, in_specs=in_specs, out_specs=out_specs, check_vma=False
    )
```

```python
import jax
import jax.numpy as jnp
from jax import lax
from jax.experimental import pallas as pl
from jax.experimental.pallas import tpu as pltpu
from jax.sharding import PartitionSpec as P


BF = jnp.bfloat16
F32 = jnp.float32
NZ = 8
NX = 4
BC = 16
REACH = ((4, 3), (3, 4))


def to_core(x):
    return lax.ppermute(x, "col", [(i, i ^ 1) for i in range(2 * NZ)])


def twisted(x, step=1):
    pairs = []
    for i in range(2 * NZ):
        z, c = i // 2, i % 2
        pairs.append((i, 2 * ((z + (step if c == 0 else -step)) % NZ) + c))
    return lax.ppermute(x, "col", pairs)


def along_z(x, step):
    return lax.ppermute(x, "col", [(i, (i + 2 * step) % (2 * NZ)) for i in range(2 * NZ)])


def along_x(x, step):
    return lax.ppermute(x, "row", [(i, (i + step) % NX) for i in range(NX)])


def exchange(x, axes):
    return lax.all_to_all(x, axes, 0, 0, tiled=True)


def pick(x, index):
    return lax.dynamic_index_in_dim(x, index, 0, keepdims=False)


def put(x, piece, index):
    return lax.dynamic_update_index_in_dim(x, piece, index, 0)


def dot(a, b):
    return jnp.dot(a, b, preferred_element_type=F32)


def root_kernel(at, home, one, two, three, four, others, a, out, x):
    z, c = at[0], at[1]
    sign = 1 - 2 * c
    n = home.shape[0]
    h = n // 2

    def place(value, chip, core):
        start = pl.multiple_of((chip & (NZ - 1)) * n + core * h, h)
        x[pl.ds(start, h), :] = value

    def pair(ref, start, chip, core):
        place(ref[start : start + h, :], chip, core)
        place(ref[start + h : start + n, :], chip, 1 - core)

    pair(home, 0, z, c)
    pair(one, 0, z - sign, c)
    pair(two, 0, z - 2 * sign, c)
    pair(three, 0, z - 3 * sign, c)
    place(four[...], z + 4, c)
    for i in range(3):
        pair(others, i * n, z + (i + 1) * sign, 1 - c)
    place(others[3 * n :, :], z + 4, 1 - c)
    out[...] = dot(x[...], a[...]).astype(BF)


def child_product(c, near, far, inverse):
    depth = near.shape[1]
    own_rows = pl.ds(pl.multiple_of(c * depth, depth), depth)
    far_rows = pl.ds(pl.multiple_of((1 - c) * depth, depth), depth)
    return (dot(near[...], inverse[own_rows, :]) + dot(far[...], inverse[far_rows, :])).astype(BF)


def first_kernel(at, near, far, inverse, out):
    out[...] = child_product(at[1], near, far, inverse)


def second_kernel(at, near, far, inverse, before, *refs):
    outs, whole = refs[:NX], refs[NX]
    block = child_product(at[1], near, far, inverse)
    n = before.shape[0] // NZ
    for i in range(NZ):
        whole[2 * i * n : (2 * i + 1) * n, :] = before[i * n : (i + 1) * n, :]
        whole[(2 * i + 1) * n : (2 * i + 2) * n, :] = block[i * n : (i + 1) * n, :]
    size = whole.shape[0] // NX
    for d in range(NX):
        start = pl.multiple_of(((at[2] + d) & (NX - 1)) * size, size)
        outs[d][...] = whole[pl.ds(start, size), :]


def local_call(kernel, shapes, inputs, flops, scratch=()):
    vmem = pl.BlockSpec(memory_space=pltpu.VMEM)
    shapes = [jax.ShapeDtypeStruct(shape, BF) for shape in shapes]
    size = sum(x.size * x.dtype.itemsize for x in (*inputs, *shapes))
    return pl.pallas_call(
        kernel,
        out_shape=shapes,
        in_specs=[pl.BlockSpec(memory_space=pltpu.SMEM)] + [vmem] * (len(inputs) - 1),
        out_specs=[vmem] * len(shapes),
        scratch_shapes=scratch,
        compiler_params=pltpu.CompilerParams(vmem_limit_bytes=16 * 2**20),
        cost_estimate=pl.CostEstimate(flops=flops, bytes_accessed=size, transcendentals=0),
    )(*inputs)


def on_device(root_rhs, root_inverse, child_rhs, child_inverse, off_diagonal, pattern):
    r = lax.axis_index("row")
    k = lax.axis_index("col")
    z = k >> 1
    c = k & 1
    first = c == 0

    height, breadth = off_diagonal.shape[1:]
    half = breadth // 2
    blocks = BC // NX
    rows = child_rhs.shape[1]
    width = child_inverse.shape[2]
    small, depth = root_rhs.shape

    other = to_core(root_rhs)
    home = jnp.concatenate([root_rhs, other])
    four = twisted(home[:small], 4)
    three = twisted(home, 3)
    two = twisted(home, 2)
    one = twisted(home, 1)
    couple_own = lax.dynamic_slice(off_diagonal[0], (0, c * half), (height, half))
    rhs_own = lax.dynamic_slice(child_rhs[0], (0, c * half), (rows, half))
    away = jnp.concatenate(
        [
            lax.dynamic_slice(off_diagonal[0], (0, (1 - c) * half), (height, half)),
            lax.dynamic_slice(child_rhs[0], (0, (1 - c) * half), (rows, half)),
        ]
    )
    away = to_core(away)
    others = to_core(jnp.concatenate([one, two, three, four]))
    couple_far = lax.optimization_barrier(
        lax.dynamic_slice(away, (z >> 3, 0), (height, half))
    )
    rhs_far = away[height:]
    rhs = lax.optimization_barrier(
        (jnp.where(first, rhs_own, rhs_far), jnp.where(first, rhs_far, rhs_own))
    )
    others, couple_far, rhs, couple_own = lax.optimization_barrier(
        (others, couple_far, rhs, couple_own)
    )
    masks = lax.dynamic_slice(pattern[0], (2 * z, r * blocks + c * (blocks // 2)), (2, blocks // 2))
    masks = jnp.repeat(masks != 0, half // (blocks // 2), axis=1)
    keep_own = jnp.where(first, masks[0], masks[1])
    keep_far = jnp.where(first, masks[1], masks[0])
    at = jnp.stack([z, c, r]).astype(jnp.int32)
    (part,) = local_call(
        root_kernel,
        [(2 * NZ * small, width)],
        (at, home, one, two, three, four, others, root_inverse),
        4 * NZ * small * depth * width,
        [pltpu.VMEM((2 * NZ * small, depth), BF)],
    )

    solved = exchange(part.reshape(NX, rows, width), "row").astype(F32).sum(0).astype(BF)
    full = jnp.broadcast_to(solved[None], (NX * NX, rows, width))
    full = exchange(full, ("layer", "row")).reshape(NX * NX * rows, width)
    full_far = to_core(full)
    update = lax.optimization_barrier(
        jnp.where(keep_own[None], dot(full, couple_own), 0.0).astype(BF)
    ).astype(F32) + jnp.where(keep_far[None], dot(full_far, couple_far), 0.0)
    update = update.astype(BF).reshape(2 * NZ, rows, half)

    def term(h, d):
        return lax.optimization_barrier(pick(update, 2 * ((z + d) & (NZ - 1)) + h))

    terms = {(h, d): term(h, d) for h in range(2) for d in range(-REACH[h][1], REACH[h][0] + 1)}
    chains = {}
    for step in range(4):
        for h in range(2):
            for way, n in zip((1, -1), REACH[h]):
                if step < n:
                    block = terms[h, way * (n - step)]
                    if step > 0:
                        block = (block.astype(F32) + chains[h, way].astype(F32)).astype(BF)
                    chains[h, way] = along_z(block, way)

    near = []
    for h in range(2):
        base = lax.optimization_barrier(rhs[h].astype(F32) - terms[h, 0].astype(F32))
        reduced = (base - (chains[h, 1].astype(F32) + chains[h, -1].astype(F32))).astype(BF)
        near.append(put(jnp.zeros((NZ, rows, half), BF), reduced, z))
        chains[h, 1] = chains[h, -1] = reduced
    for step in range(4):
        for h in range(2):
            for way, n in zip((1, -1), REACH[h]):
                if step < n:
                    chains[h, way] = along_z(chains[h, way], way)
                    near[h] = put(near[h], chains[h, way], (z - way * (step + 1)) & (NZ - 1))

    calls = (
        (first_kernel, [(NZ * rows, width)], ()),
        (second_kernel, [(4 * rows, width)] * NX, [pltpu.VMEM((2 * NZ * rows, width), BF)]),
    )
    parts = ()
    for h, (kernel, shapes, scratch) in enumerate(calls):
        gathered = near[h].reshape(NZ * rows, half)
        far = to_core(gathered)
        parts = local_call(
            kernel,
            shapes,
            (at, gathered, far, child_inverse[0], *parts),
            4 * NZ * rows * half * width,
            scratch,
        )
    total = parts[0].astype(F32)
    for step in (2, 1, 3):
        total = total + along_x(parts[step], step).astype(F32)
    child = total.astype(BF)
    return (solved, child[None])


def solution(mesh):
    in_specs = (
        P(("layer", "col"), "row"),
        P("row", "col"),
        P("layer", "col", "row"),
        P("layer", "row", "col"),
        P("layer", "col", "row"),
        P("layer", None, None),
    )
    out_specs = (P(("layer", "row"), "col"), P("layer", "row", "col"))

    return jax.shard_map(
        on_device, mesh=mesh, in_specs=in_specs, out_specs=out_specs, check_vma=False
    )
```
